512 devices in a mesh: row: 256 (over y, x, z), col: 2 (over core).
Axes of the slice: x: 4, y: 8, z: 8, core: 2. Of those that a mesh axis runs over, the one named last changes fastest.
Arguments:
- panel: float32 [131072, 2048], P('row', 'col'), may hold values from -6 to 6
- inner_vecs: float32 [256, 4, 256, 128], P('row', None, 'col'), may hold values from -0.375 to 0.375
- inner_factor: float32 [256, 4, 128, 128], P('row'), may hold values from -0.5 to 0.5
- border_vecs: float32 [256, 4, 256, 128], P('row', None, 'col'), may hold values from -0.375 to 0.375
- border_factor: float32 [256, 4, 128, 128], P('row'), may hold values from -0.5 to 0.5
- group_start: int32 [4], replicated, may hold values from 0 to 192
- group_span: int32 [4], replicated, may hold values from 63 to 255
Outputs:
- panel_out: float32 [131072, 2048], P('row', 'col')
The draws below stay inside these ranges and needn't reach their ends.
All inputs are finite; a program needn't handle non-finite values.
Results may differ from the reference program's by a relative error of at most 0.00011.
Values sent between devices are 32-bit elements; how exact they have to be, the bound alone decides.
A program may use at most 64 MiB of HBM per device.

```python
import jax
import jax.numpy as jnp
from jax import lax

NB = 128
BAND = 256
ROWS_DEV = 512
STEPS = 4
ORDER = 131072
NVEC = 2048
N_ROW = 256


def group_draw(key):
    key = jax.random.fold_in(key, 11)
    limit = N_ROW - 1
    keys = jax.random.split(key, 2 * STEPS)
    lowest = max(limit // 4, 1)
    current = jnp.array(limit, jnp.int32)
    spans = [current]
    for index in range(1, STEPS):
        if index == STEPS - 1:
            current = jnp.array(lowest, jnp.int32)
        else:
            current = jax.random.randint(keys[index], (), lowest, current + 1, dtype=jnp.int32)
        spans.append(current)
    starts = []
    for index in range(STEPS):
        if index == STEPS - 1:
            starts.append(jnp.array(limit - lowest, jnp.int32))
        else:
            starts.append(jax.random.randint(keys[STEPS + index], (), 0, limit - spans[index] + 1, dtype=jnp.int32))
    return (jnp.stack(starts).astype(jnp.int32), jnp.stack(spans).astype(jnp.int32))


def draw_group_start(key, part):
    return group_draw(key)[0]


def draw_group_span(key, part):
    return group_draw(key)[1]


def level_of(rng, extent, pieces, smallest, high):
    loudness = 1.0
    for axis_at, parts in pieces:
        draws = jax.random.uniform(jax.random.fold_in(jax.random.fold_in(rng, 6), axis_at), (parts,), jnp.float32, smallest / len(pieces), high / len(pieces))
        loudness = loudness * jnp.repeat(jnp.exp(draws), extent[axis_at] // parts).reshape((-1,) + (1,) * (len(extent) - 1 - axis_at))
    return loudness


def bell_draw(rng, shape, spread, most, cuts=(), kind=jnp.bfloat16):
    factor_of = level_of(rng, shape, cuts, -0.22, 0.18) if cuts else 1.0
    result = jax.random.normal(rng, shape, jnp.float32) * spread * factor_of
    return jnp.minimum(jnp.maximum(result, -most), most).astype(kind)


def setup_inputs(seed: int = 0) -> dict:
    key_of = jax.random.split(jax.random.key(seed), 8)
    panel = bell_draw(key_of[0], (ORDER, NVEC), 1.0, 6.0, ((0, 256), (1, 2)), jnp.float32)
    inner_vecs = bell_draw(key_of[1], (N_ROW, STEPS, BAND, NB), BAND ** -0.5, 0.375, ((0, 256), (2, 2)), jnp.float32)
    inner_factor = bell_draw(key_of[2], (N_ROW, STEPS, NB, NB), NB ** -0.5, 0.5, ((0, 256),), jnp.float32)
    border_vecs = bell_draw(key_of[3], (N_ROW, STEPS, BAND, NB), BAND ** -0.5, 0.375, ((0, 256), (2, 2)), jnp.float32)
    border_factor = bell_draw(key_of[4], (N_ROW, STEPS, NB, NB), NB ** -0.5, 0.5, ((0, 256),), jnp.float32)
    group_start = draw_group_start(jax.random.fold_in(key_of[7], 71), 0)
    group_span = draw_group_span(jax.random.fold_in(key_of[7], 71), 0)
    return dict(panel=panel, inner_vecs=inner_vecs, inner_factor=inner_factor, border_vecs=border_vecs, border_factor=border_factor, group_start=group_start, group_span=group_span)


def reflect(vectors, factor, band):
    inner = jnp.einsum("nbk,nbc->nkc", vectors, band, precision=lax.Precision.HIGHEST)
    scaled = jnp.einsum("nkj,njc->nkc", factor, inner, precision=lax.Precision.HIGHEST)
    return jnp.einsum("nbk,nkc->nbc", vectors, scaled, precision=lax.Precision.HIGHEST)


def reference(panel, inner_vecs, inner_factor, border_vecs, border_factor, group_start, group_span):
    sections = panel.reshape(N_ROW, ROWS_DEV, NVEC)
    section_ids = jnp.arange(N_ROW, dtype=jnp.int32)
    for step in range(STEPS):
        active = (section_ids >= group_start[step]) & (section_ids < group_start[step] + group_span[step])
        if step % 2 == 0:
            middle = sections[:, NB:3 * NB]
            sections = sections.at[:, NB:3 * NB].set(middle - reflect(inner_vecs[:, step], inner_factor[:, step], middle))
            band = jnp.concatenate([sections[:-1, ROWS_DEV - NB:], sections[1:, :NB]], axis=1)
            change = reflect(border_vecs[:-1, step], border_factor[:-1, step], band)
            change = jnp.where(active[:-1, None, None], change, jnp.zeros_like(change))
            sections = sections.at[:-1, ROWS_DEV - NB:].set(sections[:-1, ROWS_DEV - NB:] - change[:, :NB])
            sections = sections.at[1:, :NB].set(sections[1:, :NB] - change[:, NB:])
        else:
            upper = sections[:, :2 * NB]
            sections = sections.at[:, :2 * NB].set(upper - reflect(inner_vecs[:, step], inner_factor[:, step], upper))
            lower = sections[:, 2 * NB:]
            change = reflect(border_vecs[:, step], border_factor[:, step], lower)
            change = jnp.where(active[:, None, None], change, jnp.zeros_like(change))
            sections = sections.at[:, 2 * NB:].set(lower - change)
    return sections.reshape(ORDER, NVEC)
```

```python
import functools

import jax
import jax.numpy as jnp
from jax import lax
from jax.experimental import pallas as pl
from jax.experimental.pallas import tpu as pltpu
from jax.sharding import PartitionSpec as P

MESH = pl.DeviceIdType.MESH
F32 = jnp.float32
BF16 = jnp.bfloat16
CHUNKS = 4


def halves(value):
    high = value.astype(BF16)
    low = (value - high.astype(F32)).astype(BF16)
    return high, low


def product(a, b, dims=((1,), (0,))):
    def dot(left, right):
        return lax.dot_general(left, right, (dims, ((), ())), preferred_element_type=F32)

    return dot(a[0], b[0]) + (dot(a[0], b[1]) + dot(a[1], b[0]))


def kernel(
    rows,
    panel,
    inner_vecs,
    inner_factor,
    border_vecs,
    border_factor,
    group_start,
    group_span,
    out,
    state,
    vec_inner,
    vec_border,
    fac_inner,
    fac_border,
    q_high,
    q_low,
    lower_send,
    lower_all,
    corner_send,
    corner_all,
    above_first,
    below_first,
    above_second,
    below_second,
    share,
    raise_buf,
    load_sem,
    send_sem,
    recv_sem,
):
    row = lax.axis_index("row")
    col = lax.axis_index("col")
    height, width = panel.shape
    nb = height // 4
    chunk = width // CHUNKS
    half = nb // 2
    down = (lax.rem(row + 1, rows), col)
    up = (lax.rem(row + rows - 1, rows), col)
    mate = (row, 1 - col)
    mine = pl.ds(pl.multiple_of(col * nb, nb), nb)
    mine_half = pl.ds(pl.multiple_of(col * half, half), half)

    loads = []

    def load(src, dst):
        copy = pltpu.make_async_copy(src, dst, load_sem.at[len(loads)])
        copy.start()
        loads.append(copy)
        return copy

    load_border = [load(border_vecs.at[0, s], vec_border.at[s, mine]) for s in (0, 2, 1, 3)]
    load_fac_border = load(border_factor.at[0], fac_border)
    load_inner = load(inner_vecs.at[0], vec_inner.at[:, mine])
    load_fac_inner = load(inner_factor.at[0], fac_inner)
    load_panel = [
        load(panel.at[:, pl.ds(k * chunk, chunk)], state.at[k]) for k in range(CHUNKS)
    ]

    barrier = pltpu.get_barrier_semaphore()
    for peer in (down, up, mate):
        pl.semaphore_signal(barrier, inc=1, device_id=peer, device_id_type=MESH)
    pl.semaphore_wait(barrier, 3)

    sends = []

    def send(src, dst, peer):
        at = len(sends)
        copy = pltpu.make_async_remote_copy(
            src_ref=src,
            dst_ref=dst,
            send_sem=send_sem.at[at],
            recv_sem=recv_sem.at[at],
            device_id=peer,
            device_id_type=MESH,
        )
        copy.start()
        sends.append(copy)
        return copy

    def send_down_first(k):
        return send(
            panel.at[pl.ds(3 * nb, nb), pl.ds(k * chunk, chunk)], above_first.at[k], down
        )

    vec_from_mate = {}
    vec_from_mate[0] = send(border_vecs.at[0, 0], vec_border.at[0, mine], mate)
    down_first = [send_down_first(0)]
    up_first = [
        send(panel.at[pl.ds(0, nb), pl.ds(k * chunk, chunk)], below_first.at[k], up)
        for k in range(CHUNKS)
    ]
    vec_from_mate[2] = send(border_vecs.at[0, 2], vec_border.at[2, mine], mate)
    down_first.append(send_down_first(1))
    inner_from_mate = send(inner_vecs.at[0], vec_inner.at[:, mine], mate)
    vec_from_mate[1] = send(border_vecs.at[0, 1], vec_border.at[1, mine], mate)
    vec_from_mate[3] = send(border_vecs.at[0, 3], vec_border.at[3, mine], mate)

    def build(slot, vectors, factor, scale):
        v = halves(vectors)
        w = halves(product(v, halves(factor)))
        q = product(w, v, ((1,), (1,)))
        if scale is not None:
            q = q * scale
        high, low = halves(q)
        q_high[slot] = high
        q_low[slot] = low
        return q

    def active(s):
        start = group_start[s]
        span = group_span[s]
        return ((row >= start) & (row < start + span)).astype(F32)

    def build_border(s):
        return build(4 + s, vec_border[s], fac_border[s], active(s))

    for copy in load_border:
        copy.wait()
    load_fac_border.wait()

    vec_from_mate[0].wait_recv()
    q = build_border(0)
    lower_send[...] = q[nb:]
    vec_from_mate[2].wait_recv()
    q = build_border(2)
    corner_send[...] = q[nb:, nb:]
    lower_down = send(lower_send.at[mine_half], lower_all.at[mine_half], down)
    corner_down = send(corner_send.at[mine_half], corner_all.at[mine_half], down)
    for k in range(2, CHUNKS):
        down_first.append(send_down_first(k))

    load_inner.wait()
    load_fac_inner.wait()
    inner_from_mate.wait_recv()
    vec_from_mate[1].wait_recv()
    vec_from_mate[3].wait_recv()
    for slot in (0, 1, 2, 3):
        build(slot, vec_inner[slot], fac_inner[slot], None)
        if slot % 2 == 1:
            build_border(slot)

    def q_of(slot, r=slice(None), c=slice(None)):
        return q_high[slot, r, c], q_low[slot, r, c]

    def apply(slot, band):
        return band - product(q_of(slot), halves(band))

    up_second, down_second = [], []

    def lower_side(k):
        if k == 0:
            load_panel_wait(0)
        else:
            load_panel_wait(k)
        state[k, nb : 3 * nb] = apply(0, state[k, nb : 3 * nb])
        up_first[k].wait_recv()
        last = state[k, 3 * nb :]
        band = jnp.concatenate([last, below_first[k]], axis=0)
        last = last - product(q_of(4, slice(0, nb)), halves(band))
        band = jnp.concatenate([state[k, 2 * nb : 3 * nb], last], axis=0)
        band = apply(5, band)
        state[k, 2 * nb :] = band
        share[k] = product(q_of(6, slice(nb, None), slice(0, nb)), halves(band[nb:]))

    def load_panel_wait(k):
        load_panel[k].wait()

    def send_share(k):
        down_second.append(send(share.at[k], above_second.at[k], down))

    def upper_side(k):
        down_first[k].wait_recv()
        first = state[k, :nb]
        band = jnp.concatenate([above_first[k], first], axis=0)
        first = first - product(halves(lower_all[...]), halves(band))
        band = jnp.concatenate([first, state[k, nb : 2 * nb]], axis=0)
        band = apply(1, band)
        state[k, : 2 * nb] = band
        raise_buf[k] = band[:nb]

    def send_raise(k):
        up_second.append(send(raise_buf.at[k], below_second.at[k], up))

    def middle(k):
        state[k, nb : 3 * nb] = apply(2, state[k, nb : 3 * nb])

    def finish(k):
        down_second[k].wait_recv()
        first = state[k, :nb]
        first = first - (product(halves(corner_all[...]), halves(first)) + above_second[k])
        band = jnp.concatenate([first, state[k, nb : 2 * nb]], axis=0)
        out[: 2 * nb, k * chunk : (k + 1) * chunk] = apply(3, band)
        up_second[k].wait_recv()
        last = state[k, 3 * nb :]
        band = jnp.concatenate([last, below_second[k]], axis=0)
        last = last - product(q_of(6, slice(0, nb)), halves(band))
        band = jnp.concatenate([state[k, 2 * nb : 3 * nb], last], axis=0)
        out[2 * nb :, k * chunk : (k + 1) * chunk] = apply(7, band)

    lower_side(0)
    lower_side(1)
    send_share(0)
    lower_down.wait_recv()
    corner_down.wait_recv()
    lower_pair = send(lower_all.at[mine_half], lower_all.at[mine_half], mate)
    corner_pair = send(corner_all.at[mine_half], corner_all.at[mine_half], mate)
    lower_pair.wait_recv()
    corner_pair.wait_recv()
    upper_side(0)
    send_share(1)
    upper_side(1)
    send_raise(0)
    lower_side(2)
    send_raise(1)
    upper_side(2)
    send_share(2)
    lower_side(3)
    send_raise(2)
    upper_side(3)
    send_share(3)
    middle(0)
    send_raise(3)
    for k in range(1, CHUNKS):
        middle(k)
    for k in range(CHUNKS):
        finish(k)
    for copy in sends:
        copy.wait_send()


def local(panel, inner_vecs, inner_factor, border_vecs, border_factor, group_start, group_span, *, rows):
    height, width = panel.shape
    nb = height // 4
    chunk = width // CHUNKS
    steps = inner_factor.shape[1]
    vmem, dma = pltpu.VMEM, pltpu.SemaphoreType.DMA
    anywhere = pl.BlockSpec(memory_space=pl.ANY)
    scalars = pl.BlockSpec(memory_space=pltpu.SMEM)
    copies = 4 * CHUNKS + 5 + 4
    return pl.pallas_call(
        functools.partial(kernel, rows),
        out_shape=jax.ShapeDtypeStruct(panel.shape, F32),
        in_specs=[anywhere] * 5 + [scalars] * 2,
        out_specs=pl.BlockSpec(memory_space=pltpu.VMEM),
        scratch_shapes=[
            vmem((CHUNKS, height, chunk), F32),
            vmem((steps, 2 * nb, nb), F32),
            vmem((steps, 2 * nb, nb), F32),
            vmem((steps, nb, nb), F32),
            vmem((steps, nb, nb), F32),
            vmem((2 * steps, 2 * nb, 2 * nb), BF16),
            vmem((2 * steps, 2 * nb, 2 * nb), BF16),
            vmem((nb, 2 * nb), F32),
            vmem((nb, 2 * nb), F32),
            vmem((nb, nb), F32),
            vmem((nb, nb), F32),
            vmem((CHUNKS, nb, chunk), F32),
            vmem((CHUNKS, nb, chunk), F32),
            vmem((CHUNKS, nb, chunk), F32),
            vmem((CHUNKS, nb, chunk), F32),
            vmem((CHUNKS, nb, chunk), F32),
            vmem((CHUNKS, nb, chunk), F32),
            dma((7 + CHUNKS,)),
            dma((copies,)),
            dma((copies,)),
        ],
        compiler_params=pltpu.CompilerParams(
            collective_id=0, has_side_effects=True, vmem_limit_bytes=48 * 2**20
        ),
        name="diamonds",
    )(panel, inner_vecs, inner_factor, border_vecs, border_factor, group_start, group_span)


def solution(mesh):
    placed = (
        P("row", "col"),
        P("row", None, "col", None),
        P("row", None, None, None),
        P("row", None, "col", None),
        P("row", None, None, None),
        P(),
        P(),
    )
    return jax.shard_map(
        functools.partial(local, rows=mesh.shape["row"]),
        mesh=mesh,
        in_specs=placed,
        out_specs=P("row", "col"),
        check_vma=False,
    )
```

```python
import functools

import jax
import jax.numpy as jnp
from jax import lax
from jax.experimental import pallas as pl
from jax.experimental.pallas import tpu as pltpu
from jax.sharding import PartitionSpec as P

MESH = pl.DeviceIdType.MESH
F32 = jnp.float32
BF16 = jnp.bfloat16
CHUNKS = 4


def halves(value):
    high = value.astype(BF16)
    low = (value - high.astype(F32)).astype(BF16)
    return high, low


def product(a, b, dims=((1,), (0,))):
    def dot(left, right):
        return lax.dot_general(left, right, (dims, ((), ())), preferred_element_type=F32)

    return dot(a[0], b[0]) + (dot(a[0], b[1]) + dot(a[1], b[0]))


def kernel(
    rows,
    panel,
    inner_vecs,
    inner_factor,
    border_vecs,
    border_factor,
    group_start,
    group_span,
    out,
    state,
    vec_inner,
    vec_border,
    fac_inner,
    fac_border,
    q_high,
    q_low,
    lower_send,
    lower_all,
    corner_send,
    corner_all,
    above_first,
    below_first,
    above_second,
    below_second,
    share,
    raise_buf,
    start_ref,
    span_ref,
    load_sem,
    send_sem,
    recv_sem,
):
    row = lax.axis_index("row")
    col = lax.axis_index("col")
    height, width = panel.shape
    nb = height // 4
    chunk = width // CHUNKS
    half = nb // 2
    has_up, has_down = row > 0, row < rows - 1
    down = (jnp.minimum(row + 1, rows - 1), col)
    up = (jnp.maximum(row - 1, 0), col)
    mate = (row, 1 - col)
    mine = pl.ds(pl.multiple_of(col * nb, nb), nb)
    mine_half = pl.ds(pl.multiple_of(col * half, half), half)

    loads = []

    def load(src, dst):
        copy = pltpu.make_async_copy(src, dst, load_sem.at[len(loads)])
        copy.start()
        loads.append(copy)
        return copy

    load_border = [load(border_vecs.at[0, s], vec_border.at[s, mine]) for s in (0, 2, 1, 3)]
    load_fac_border = load(border_factor.at[0], fac_border)
    load_inner = load(inner_vecs.at[0], vec_inner.at[:, mine])
    load_fac_inner = load(inner_factor.at[0], fac_inner)
    load_panel = [
        load(panel.at[:, pl.ds(k * chunk, chunk)], state.at[k]) for k in range(CHUNKS)
    ]

    load_start = load(group_start, start_ref)
    load_span = load(group_span, span_ref)

    barrier = pltpu.get_barrier_semaphore()

    def greet(peer):
        pl.semaphore_signal(barrier, inc=1, device_id=peer, device_id_type=MESH)

    pl.when(has_up)(lambda: greet(up))
    pl.when(has_down)(lambda: greet(down))
    greet(mate)

    @pl.when(jnp.logical_not(has_up))
    def _():
        lower_all[...] = jnp.zeros_like(lower_all)
        corner_all[...] = jnp.zeros_like(corner_all)
        above_first[...] = jnp.zeros_like(above_first)
        above_second[...] = jnp.zeros_like(above_second)

    @pl.when(jnp.logical_not(has_down))
    def _():
        below_first[...] = jnp.zeros_like(below_first)
        below_second[...] = jnp.zeros_like(below_second)

    pl.semaphore_wait(barrier, 1 + has_up.astype(jnp.int32) + has_down.astype(jnp.int32))

    sends = []

    class Send:
        def __init__(self, src, dst, peer, given, taken):
            at = len(sends)
            self.given, self.taken = given, taken
            self.copy = pltpu.make_async_remote_copy(
                src_ref=src,
                dst_ref=dst,
                send_sem=send_sem.at[at],
                recv_sem=recv_sem.at[at],
                device_id=peer,
                device_id_type=MESH,
            )
            self.on(given, self.copy.start)
            sends.append(self)

        def on(self, condition, action):
            if condition is None:
                action()
            else:
                pl.when(condition)(lambda: action())

        def wait_recv(self):
            self.on(self.taken, self.copy.wait_recv)

        def wait_send(self):
            self.on(self.given, self.copy.wait_send)

    def send(src, dst, to):
        if to == "mate":
            return Send(src, dst, mate, None, None)
        if to == "down":
            return Send(src, dst, down, has_down, has_up)
        return Send(src, dst, up, has_up, has_down)

    def send_down_first(k):
        return send(
            panel.at[pl.ds(3 * nb, nb), pl.ds(k * chunk, chunk)], above_first.at[k], "down"
        )

    vec_from_mate = {}
    vec_from_mate[0] = send(border_vecs.at[0, 0], vec_border.at[0, mine], "mate")
    down_first = [send_down_first(0)]
    up_first = [
        send(panel.at[pl.ds(0, nb), pl.ds(k * chunk, chunk)], below_first.at[k], "up")
        for k in range(CHUNKS)
    ]
    vec_from_mate[2] = send(border_vecs.at[0, 2], vec_border.at[2, mine], "mate")
    down_first.append(send_down_first(1))
    inner_from_mate = send(inner_vecs.at[0], vec_inner.at[:, mine], "mate")
    vec_from_mate[1] = send(border_vecs.at[0, 1], vec_border.at[1, mine], "mate")
    vec_from_mate[3] = send(border_vecs.at[0, 3], vec_border.at[3, mine], "mate")

    def build(slot, vectors, factor, scale):
        v = halves(vectors)
        w = halves(product(v, halves(factor)))
        q = product(w, v, ((1,), (1,)))
        if scale is not None:
            q = q * scale
        high, low = halves(q)
        q_high[slot] = high
        q_low[slot] = low
        return q

    def active(s):
        start = start_ref[s]
        span = span_ref[s]
        return ((row >= start) & (row < start + span)).astype(F32)

    def build_border(s):
        return build(4 + s, vec_border[s], fac_border[s], active(s))

    for copy in load_border:
        copy.wait()
    load_fac_border.wait()
    load_start.wait()
    load_span.wait()

    vec_from_mate[0].wait_recv()
    q = build_border(0)
    lower_send[...] = q[nb:]
    vec_from_mate[2].wait_recv()
    q = build_border(2)
    corner_send[...] = q[nb:, nb:]
    lower_down = send(lower_send.at[mine_half], lower_all.at[mine_half], "down")
    corner_down = send(corner_send.at[mine_half], corner_all.at[mine_half], "down")
    for k in range(2, CHUNKS):
        down_first.append(send_down_first(k))

    load_inner.wait()
    load_fac_inner.wait()
    inner_from_mate.wait_recv()
    vec_from_mate[1].wait_recv()
    vec_from_mate[3].wait_recv()
    for slot in (0, 1, 2, 3):
        build(slot, vec_inner[slot], fac_inner[slot], None)
        if slot % 2 == 1:
            build_border(slot)

    def q_of(slot, r=slice(None), c=slice(None)):
        return q_high[slot, r, c], q_low[slot, r, c]

    def apply(slot, band):
        return band - product(q_of(slot), halves(band))

    up_second, down_second = [], []

    def lower_side(k):
        load_panel[k].wait()
        state[k, nb : 3 * nb] = apply(0, state[k, nb : 3 * nb])
        up_first[k].wait_recv()
        last = state[k, 3 * nb :]
        band = jnp.concatenate([last, below_first[k]], axis=0)
        last = last - product(q_of(4, slice(0, nb)), halves(band))
        band = jnp.concatenate([state[k, 2 * nb : 3 * nb], last], axis=0)
        band = apply(5, band)
        state[k, 2 * nb :] = band
        share[k] = product(q_of(6, slice(nb, None), slice(0, nb)), halves(band[nb:]))

    def send_share(k):
        down_second.append(send(share.at[k], above_second.at[k], "down"))

    def upper_side(k):
        down_first[k].wait_recv()
        first = state[k, :nb]
        band = jnp.concatenate([above_first[k], first], axis=0)
        first = first - product(halves(lower_all[...]), halves(band))
        band = jnp.concatenate([first, state[k, nb : 2 * nb]], axis=0)
        band = apply(1, band)
        state[k, : 2 * nb] = band
        raise_buf[k] = band[:nb]

    def send_raise(k):
        up_second.append(send(raise_buf.at[k], below_second.at[k], "up"))

    def middle(k):
        state[k, nb : 3 * nb] = apply(2, state[k, nb : 3 * nb])

    def finish_upper(k):
        down_second[k].wait_recv()
        first = state[k, :nb]
        first = first - (product(halves(corner_all[...]), halves(first)) + above_second[k])
        band = jnp.concatenate([first, state[k, nb : 2 * nb]], axis=0)
        out[: 2 * nb, k * chunk : (k + 1) * chunk] = apply(3, band)

    def finish_lower(k):
        up_second[k].wait_recv()
        last = state[k, 3 * nb :]
        band = jnp.concatenate([last, below_second[k]], axis=0)
        last = last - product(q_of(6, slice(0, nb)), halves(band))
        band = jnp.concatenate([state[k, 2 * nb : 3 * nb], last], axis=0)
        out[2 * nb :, k * chunk : (k + 1) * chunk] = apply(7, band)

    lower_side(0)
    lower_side(1)
    send_share(0)
    lower_down.wait_recv()
    corner_down.wait_recv()
    lower_pair = send(lower_all.at[mine_half], lower_all.at[mine_half], "mate")
    corner_pair = send(corner_all.at[mine_half], corner_all.at[mine_half], "mate")
    lower_pair.wait_recv()
    corner_pair.wait_recv()
    upper_side(0)
    send_share(1)
    upper_side(1)
    send_raise(0)
    lower_side(2)
    send_raise(1)
    upper_side(2)
    send_share(2)
    lower_side(3)
    send_raise(2)
    upper_side(3)
    send_share(3)
    middle(0)
    send_raise(3)
    for k in range(1, CHUNKS):
        middle(k)
    finish_lower(0)
    for k in range(1, CHUNKS):
        finish_lower(k)
        finish_upper(k - 1)
    finish_upper(CHUNKS - 1)
    for copy in sends:
        copy.wait_send()


def local(panel, inner_vecs, inner_factor, border_vecs, border_factor, group_start, group_span, *, rows):
    height, width = panel.shape
    nb = height // 4
    chunk = width // CHUNKS
    steps = inner_factor.shape[1]
    vmem, dma = pltpu.VMEM, pltpu.SemaphoreType.DMA
    anywhere = pl.BlockSpec(memory_space=pltpu.HBM)
    copies = 4 * CHUNKS + 5 + 4
    return pl.pallas_call(
        functools.partial(kernel, rows),
        out_shape=jax.ShapeDtypeStruct(panel.shape, F32),
        in_specs=[anywhere] * 7,
        out_specs=pl.BlockSpec(memory_space=pltpu.VMEM),
        scratch_shapes=[
            vmem((CHUNKS, height, chunk), F32),
            vmem((steps, 2 * nb, nb), F32),
            vmem((steps, 2 * nb, nb), F32),
            vmem((steps, nb, nb), F32),
            vmem((steps, nb, nb), F32),
            vmem((2 * steps, 2 * nb, 2 * nb), BF16),
            vmem((2 * steps, 2 * nb, 2 * nb), BF16),
            vmem((nb, 2 * nb), F32),
            vmem((nb, 2 * nb), F32),
            vmem((nb, nb), F32),
            vmem((nb, nb), F32),
            vmem((CHUNKS, nb, chunk), F32),
            vmem((CHUNKS, nb, chunk), F32),
            vmem((CHUNKS, nb, chunk), F32),
            vmem((CHUNKS, nb, chunk), F32),
            vmem((CHUNKS, nb, chunk), F32),
            vmem((CHUNKS, nb, chunk), F32),
            pltpu.SMEM((steps,), jnp.int32),
            pltpu.SMEM((steps,), jnp.int32),
            dma((9 + CHUNKS,)),
            dma((copies,)),
            dma((copies,)),
        ],
        compiler_params=pltpu.CompilerParams(
            collective_id=0, has_side_effects=True, vmem_limit_bytes=48 * 2**20
        ),
        name="diamonds",
    )(
        *(
            pltpu.with_memory_space_constraint(a, pltpu.HBM)
            for a in (
                panel,
                inner_vecs,
                inner_factor,
                border_vecs,
                border_factor,
                group_start,
                group_span,
            )
        )
    )


def solution(mesh):
    placed = (
        P("row", "col"),
        P("row", None, "col", None),
        P("row", None, None, None),
        P("row", None, "col", None),
        P("row", None, None, None),
        P(),
        P(),
    )
    return jax.shard_map(
        functools.partial(local, rows=mesh.shape["row"]),
        mesh=mesh,
        in_specs=placed,
        out_specs=P("row", "col"),
        check_vma=False,
    )
```

```python
import functools

import jax
import jax.numpy as jnp
from jax import lax
from jax.experimental import pallas as pl
from jax.experimental.pallas import tpu as pltpu
from jax.sharding import PartitionSpec as P

MESH = pl.DeviceIdType.MESH
F32 = jnp.float32
BF16 = jnp.bfloat16
CHUNKS = 4
EXTENT_Z = 8


def halves(value):
    high = value.astype(BF16)
    low = (value - high.astype(F32)).astype(BF16)
    return high, low


def product(a, b, dims=((1,), (0,))):
    def dot(left, right):
        return lax.dot_general(left, right, (dims, ((), ())), preferred_element_type=F32)

    return dot(a[0], b[0]) + (dot(a[0], b[1]) + dot(a[1], b[0]))


def both(*conditions):
    return functools.reduce(jnp.logical_and, conditions)


def on(condition, action):
    if condition is None:
        action()
    else:
        pl.when(condition)(lambda: action())


def kernel(
    rows,
    panel,
    inner_vecs,
    inner_factor,
    border_vecs,
    border_factor,
    group_start,
    group_span,
    out,
    state,
    vec_inner,
    vec_border,
    fac_inner,
    fac_border,
    q_high,
    q_low,
    lower_send,
    lower_all,
    corner_send,
    corner_all,
    above_first,
    below_first,
    above_second,
    below_second,
    share,
    raise_buf,
    start_ref,
    span_ref,
    load_sem,
    send_sem,
    recv_sem,
):
    row = lax.axis_index("row")
    col = lax.axis_index("col")
    height, width = panel.shape
    nb = height // 4
    chunk = width // CHUNKS
    half = nb // 2
    last = CHUNKS - 1
    z = lax.rem(row, EXTENT_Z)
    has_up, has_down = row > 0, row < rows - 1
    down = (jnp.minimum(row + 1, rows - 1), col)
    up = (jnp.maximum(row - 1, 0), col)
    mate = (row, 1 - col)
    top = z == 0
    mine = pl.ds(pl.multiple_of(col * nb, nb), nb)
    mine_half = pl.ds(pl.multiple_of(col * half, half), half)

    barrier = pltpu.get_barrier_semaphore()

    def greet(peer):
        pl.semaphore_signal(barrier, inc=1, device_id=peer, device_id_type=MESH)

    on(has_up, lambda: greet(up))
    on(has_down, lambda: greet(down))
    greet(mate)
    loads = []

    def load(src, dst):
        copy = pltpu.make_async_copy(src, dst, load_sem.at[len(loads)])
        copy.start()
        loads.append(copy)
        return copy

    load_border = load(border_vecs.at[0], vec_border.at[:, mine])
    load_fac_border = load(border_factor.at[0], fac_border)
    load_start = load(group_start, start_ref)
    load_span = load(group_span, span_ref)
    load_inner = load(inner_vecs.at[0], vec_inner.at[:, mine])
    load_fac_inner = load(inner_factor.at[0], fac_inner)
    load_panel = load(panel, state)

    @pl.when(jnp.logical_not(has_up))
    def _():
        lower_all[...] = jnp.zeros_like(lower_all)
        corner_all[...] = jnp.zeros_like(corner_all)
        above_first[...] = jnp.zeros_like(above_first)
        above_second[...] = jnp.zeros_like(above_second)

    @pl.when(jnp.logical_not(has_down))
    def _():
        below_first[...] = jnp.zeros_like(below_first)
        below_second[...] = jnp.zeros_like(below_second)

    def one(condition):
        return condition.astype(jnp.int32)

    pl.semaphore_wait(barrier, 1 + one(has_up) + one(has_down))

    sends = []

    class Send:
        def __init__(self, src, dst, peer, given, taken):
            self.given, self.taken = given, taken
            index = len(sends)
            self.copy = pltpu.make_async_remote_copy(
                src_ref=src,
                dst_ref=dst,
                send_sem=send_sem.at[index],
                recv_sem=recv_sem.at[index],
                device_id=peer,
                device_id_type=MESH,
            )
            sends.append(self)

        def start(self):
            on(self.given, self.copy.start)

        def wait_recv(self):
            on(self.taken, self.copy.wait_recv)

        def wait_send(self):
            on(self.given, self.copy.wait_send)

    def to_mate(src, dst):
        return Send(src, dst, mate, None, None)

    def to_down(src, dst, given=has_down, taken=has_up):
        return Send(src, dst, down, given, taken)

    def to_up(src, dst):
        return Send(src, dst, up, has_up, has_down)

    def border_rows(k, at_row, count):
        return panel.at[pl.ds(3 * nb + at_row, count), pl.ds(k * chunk, chunk)]

    down_first = [
        to_down(border_rows(k, 0, nb), above_first.at[k]) for k in range(CHUNKS)
    ]
    up_first = [
        to_up(panel.at[pl.ds(0, nb), pl.ds(k * chunk, chunk)], below_first.at[k])
        for k in range(CHUNKS)
    ]
    border_from_mate = [
        to_mate(border_vecs.at[0, pl.ds(s, n)], vec_border.at[pl.ds(s, n), mine])
        for s, n in ((0, 1), (1, 3))
    ]
    inner_from_mate = to_mate(inner_vecs.at[0], vec_inner.at[:, mine])
    lower_down = to_down(lower_send.at[mine_half], lower_all.at[mine_half])
    corner_down = to_down(corner_send.at[mine_half], corner_all.at[mine_half])
    lower_pair = to_mate(lower_all.at[mine_half], lower_all.at[mine_half])
    corner_pair = to_mate(corner_all.at[mine_half], corner_all.at[mine_half])
    down_second = [to_down(share.at[k], above_second.at[k]) for k in range(CHUNKS)]
    up_second = [to_up(raise_buf.at[k], below_second.at[k]) for k in range(CHUNKS)]

    down_first[0].start()
    border_from_mate[0].start()
    for copy in up_first:
        copy.start()
    border_from_mate[1].start()
    down_first[1].start()
    inner_from_mate.start()

    def build(slot, vectors, factor, scale):
        v = halves(vectors)
        w = halves(product(v, halves(factor)))
        q = product(w, v, ((1,), (1,)))
        if scale is not None:
            q = q * scale
        high, low = halves(q)
        q_high[slot] = high
        q_low[slot] = low
        return q

    def active(s):
        start = start_ref[s]
        span = span_ref[s]
        return ((row >= start) & (row < start + span)).astype(F32)

    def build_border(s):
        return build(4 + s, vec_border[s], fac_border[s], active(s))

    load_border.wait()
    load_fac_border.wait()
    load_start.wait()
    load_span.wait()

    border_from_mate[0].wait_recv()
    q = build_border(0)
    lower_send[...] = q[nb:]
    border_from_mate[1].wait_recv()
    q = build_border(2)
    corner_send[...] = q[nb:, nb:]
    lower_down.start()
    load_inner.wait()
    load_fac_inner.wait()
    inner_from_mate.wait_recv()
    build(0, vec_inner[0], fac_inner[0], None)
    corner_down.start()
    for copy in down_first[2:]:
        copy.start()

    build_border(1)
    for slot in (1, 2, 3):
        build(slot, vec_inner[slot], fac_inner[slot], None)
    build_border(3)

    def q_of(slot, r=slice(None), c=slice(None)):
        return q_high[slot, r, c], q_low[slot, r, c]

    def apply(slot, band):
        return band - product(q_of(slot), halves(band))

    load_panel.wait()

    def span_of(k):
        return slice(k * chunk, (k + 1) * chunk)

    def lower_side(k):
        state[nb : 3 * nb, span_of(k)] = apply(0, state[nb : 3 * nb, span_of(k)])
        up_first[k].wait_recv()
        end = state[3 * nb :, span_of(k)]
        band = jnp.concatenate([end, below_first[k]], axis=0)
        end = end - product(q_of(4, slice(0, nb)), halves(band))
        band = jnp.concatenate([state[2 * nb : 3 * nb, span_of(k)], end], axis=0)
        band = apply(5, band)
        share[k] = product(q_of(6, slice(nb, None), slice(0, nb)), halves(band[nb:]))
        state[2 * nb :, span_of(k)] = band

    def upper_side(k):
        down_first[k].wait_recv()
        first = state[:nb, span_of(k)]
        band = jnp.concatenate([above_first[k], first], axis=0)
        first = first - product(halves(lower_all[...]), halves(band))
        band = jnp.concatenate([first, state[nb : 2 * nb, span_of(k)]], axis=0)
        band = apply(1, band)
        raise_buf[k] = band[:nb]
        state[: 2 * nb, span_of(k)] = band

    def middle(k):
        state[nb : 3 * nb, span_of(k)] = apply(2, state[nb : 3 * nb, span_of(k)])
        first = state[:nb, span_of(k)]
        state[:nb, span_of(k)] = first - product(halves(corner_all[...]), halves(first))

    def finish_upper(k):
        down_second[k].wait_recv()
        first = state[:nb, span_of(k)] - above_second[k]
        band = jnp.concatenate([first, state[nb : 2 * nb, span_of(k)]], axis=0)
        out[: 2 * nb, span_of(k)] = apply(3, band)

    def finish_lower(k):
        up_second[k].wait_recv()
        end = state[3 * nb :, span_of(k)]
        band = jnp.concatenate([end, below_second[k]], axis=0)
        end = end - product(q_of(6, slice(0, nb)), halves(band))
        band = jnp.concatenate([state[2 * nb : 3 * nb, span_of(k)], end], axis=0)
        out[2 * nb :, span_of(k)] = apply(7, band)

    def weights():
        lower_down.wait_recv()
        lower_pair.start()
        corner_down.wait_recv()
        corner_pair.start()
        lower_pair.wait_recv()
        corner_pair.wait_recv()

    def sent_down(k):
        down_second[k].start()

    def sent_up(k):
        up_second[k].start()

    def early():
        for k in range(CHUNKS):
            lower_side(k)
            sent_down(k)
        weights()
        for k in range(CHUNKS):
            upper_side(k)
            sent_up(k)

    def usual():
        for k in range(CHUNKS):
            lower_side(k)
            sent_down(k)
            if k == 0:
                weights()
            upper_side(k)
            sent_up(k)

    pl.when(top)(early)
    pl.when(jnp.logical_not(top))(usual)
    for k in range(CHUNKS):
        middle(k)
    finish_lower(0)
    for k in range(1, CHUNKS):
        finish_lower(k)
        finish_upper(k - 1)
    finish_upper(last)
    for copy in sends:
        copy.wait_send()


def local(panel, inner_vecs, inner_factor, border_vecs, border_factor, group_start, group_span, *, rows):
    height, width = panel.shape
    nb = height // 4
    chunk = width // CHUNKS
    steps = inner_factor.shape[1]
    vmem, dma = pltpu.VMEM, pltpu.SemaphoreType.DMA
    anywhere = pl.BlockSpec(memory_space=pl.ANY)
    copies = 4 * CHUNKS + 7
    operands = (
        panel,
        inner_vecs,
        inner_factor,
        border_vecs,
        border_factor,
        group_start,
        group_span,
    )
    result = pl.pallas_call(
        functools.partial(kernel, rows),
        out_shape=jax.ShapeDtypeStruct(panel.shape, F32),
        in_specs=[pl.BlockSpec(memory_space=pltpu.HBM)] * 7,
        out_specs=pl.BlockSpec(memory_space=pltpu.VMEM),
        scratch_shapes=[
            vmem((height, width), F32),
            vmem((steps, 2 * nb, nb), F32),
            vmem((steps, 2 * nb, nb), F32),
            vmem((steps, nb, nb), F32),
            vmem((steps, nb, nb), F32),
            vmem((2 * steps, 2 * nb, 2 * nb), BF16),
            vmem((2 * steps, 2 * nb, 2 * nb), BF16),
            vmem((nb, 2 * nb), F32),
            vmem((nb, 2 * nb), F32),
            vmem((nb, nb), F32),
            vmem((nb, nb), F32),
            vmem((CHUNKS, nb, chunk), F32),
            vmem((CHUNKS, nb, chunk), F32),
            vmem((CHUNKS, nb, chunk), F32),
            vmem((CHUNKS, nb, chunk), F32),
            vmem((CHUNKS, nb, chunk), F32),
            vmem((CHUNKS, nb, chunk), F32),
            pltpu.SMEM((steps,), jnp.int32),
            pltpu.SMEM((steps,), jnp.int32),
            dma((7,)),
            dma((copies,)),
            dma((copies,)),
        ],
        compiler_params=pltpu.CompilerParams(
            collective_id=0, has_side_effects=True, vmem_limit_bytes=48 * 2**20
        ),
        name="diamonds",
    )(*(pltpu.with_memory_space_constraint(a, pltpu.HBM) for a in operands))
    return result


def solution(mesh):
    placed = (
        P("row", "col"),
        P("row", None, "col", None),
        P("row", None, None, None),
        P("row", None, "col", None),
        P("row", None, None, None),
        P(),
        P(),
    )
    return jax.shard_map(
        functools.partial(local, rows=mesh.shape["row"]),
        mesh=mesh,
        in_specs=placed,
        out_specs=P("row", "col"),
        check_vma=False,
    )
```

```python
import functools

import jax
import jax.numpy as jnp
from jax import lax
from jax.experimental import pallas as pl
from jax.experimental.pallas import tpu as pltpu
from jax.sharding import PartitionSpec as P

MESH = pl.DeviceIdType.MESH
F32 = jnp.float32
BF16 = jnp.bfloat16
CHUNKS = 4
EXTENT_Z = 8


def halves(value):
    high = value.astype(BF16)
    low = (value - high.astype(F32)).astype(BF16)
    return high, low


def product(a, b, dims=((1,), (0,))):
    def dot(left, right):
        return lax.dot_general(left, right, (dims, ((), ())), preferred_element_type=F32)

    return dot(a[0], b[0]) + (dot(a[0], b[1]) + dot(a[1], b[0]))


def both(*conditions):
    return functools.reduce(jnp.logical_and, conditions)


def on(condition, action):
    if condition is None:
        action()
    else:
        pl.when(condition)(lambda: action())


def kernel(
    rows,
    panel,
    inner_vecs,
    inner_factor,
    border_vecs,
    border_factor,
    group_start,
    group_span,
    out,
    state,
    vec_inner,
    vec_border,
    fac_inner,
    fac_border,
    q_high,
    q_low,
    lower_send,
    lower_all,
    corner_send,
    corner_all,
    above_first,
    below_first,
    above_second,
    below_second,
    share,
    raise_buf,
    start_ref,
    span_ref,
    load_sem,
    send_sem,
    recv_sem,
):
    row = lax.axis_index("row")
    col = lax.axis_index("col")
    height, width = panel.shape
    nb = height // 4
    chunk = width // CHUNKS
    half = nb // 2
    last = CHUNKS - 1
    z = lax.rem(row, EXTENT_Z)
    has_up, has_down = row > 0, row < rows - 1
    down = (jnp.minimum(row + 1, rows - 1), col)
    up = (jnp.maximum(row - 1, 0), col)
    mate = (row, 1 - col)
    top = z == 0
    mine = pl.ds(pl.multiple_of(col * nb, nb), nb)
    mine_half = pl.ds(pl.multiple_of(col * half, half), half)

    barrier = pltpu.get_barrier_semaphore()

    def greet(peer):
        pl.semaphore_signal(barrier, inc=1, device_id=peer, device_id_type=MESH)

    on(has_up, lambda: greet(up))
    on(has_down, lambda: greet(down))
    greet(mate)
    loads = []

    def load(src, dst):
        copy = pltpu.make_async_copy(src, dst, load_sem.at[len(loads)])
        copy.start()
        loads.append(copy)
        return copy

    load_border = load(border_vecs.at[0], vec_border.at[:, mine])
    load_fac_border = load(border_factor.at[0], fac_border)
    load_start = load(group_start, start_ref)
    load_span = load(group_span, span_ref)
    load_inner = load(inner_vecs.at[0], vec_inner.at[:, mine])
    load_fac_inner = load(inner_factor.at[0], fac_inner)
    load_panel = load(panel, state)

    @pl.when(jnp.logical_not(has_up))
    def _():
        lower_all[...] = jnp.zeros_like(lower_all)
        corner_all[...] = jnp.zeros_like(corner_all)
        above_first[...] = jnp.zeros_like(above_first)
        above_second[...] = jnp.zeros_like(above_second)

    @pl.when(jnp.logical_not(has_down))
    def _():
        below_first[...] = jnp.zeros_like(below_first)
        below_second[...] = jnp.zeros_like(below_second)

    def one(condition):
        return condition.astype(jnp.int32)

    pl.semaphore_wait(barrier, 1 + one(has_up) + one(has_down))

    sends = []

    class Send:
        def __init__(self, src, dst, peer, given, taken):
            self.given, self.taken = given, taken
            index = len(sends)
            self.copy = pltpu.make_async_remote_copy(
                src_ref=src,
                dst_ref=dst,
                send_sem=send_sem.at[index],
                recv_sem=recv_sem.at[index],
                device_id=peer,
                device_id_type=MESH,
            )
            sends.append(self)

        def start(self):
            on(self.given, self.copy.start)

        def wait_recv(self):
            on(self.taken, self.copy.wait_recv)

        def wait_send(self):
            on(self.given, self.copy.wait_send)

    def to_mate(src, dst):
        return Send(src, dst, mate, None, None)

    def to_down(src, dst, given=has_down, taken=has_up):
        return Send(src, dst, down, given, taken)

    def to_up(src, dst):
        return Send(src, dst, up, has_up, has_down)

    def border_rows(k, at_row, count):
        return panel.at[pl.ds(3 * nb + at_row, count), pl.ds(k * chunk, chunk)]

    down_first = [
        to_down(border_rows(k, 0, nb), above_first.at[k]) for k in range(CHUNKS)
    ]
    up_first = [
        to_up(panel.at[pl.ds(0, nb), pl.ds(k * chunk, chunk)], below_first.at[k])
        for k in range(CHUNKS)
    ]
    border_from_mate = [
        to_mate(border_vecs.at[0, pl.ds(s, n)], vec_border.at[pl.ds(s, n), mine])
        for s, n in ((0, 1), (1, 3))
    ]
    inner_from_mate = to_mate(inner_vecs.at[0], vec_inner.at[:, mine])
    lower_down = to_down(lower_send.at[mine_half], lower_all.at[mine_half])
    corner_down = to_down(corner_send.at[mine_half], corner_all.at[mine_half])
    lower_pair = to_mate(lower_all.at[mine_half], lower_all.at[mine_half])
    corner_pair = to_mate(corner_all.at[mine_half], corner_all.at[mine_half])
    down_second = [to_down(share.at[k], above_second.at[k]) for k in range(CHUNKS)]
    up_second = [to_up(raise_buf.at[k], below_second.at[k]) for k in range(CHUNKS)]

    down_first[0].start()
    border_from_mate[0].start()
    for copy in up_first:
        copy.start()
    border_from_mate[1].start()
    inner_from_mate.start()

    def build(slot, vectors, factor, scale, keep=None):
        v = halves(vectors)
        w = halves(product(v, halves(factor)))
        q = product(w, v, ((1,), (1,)))
        if scale is not None:
            q = q * scale
        if keep is not None:
            keep(q)
        high, low = halves(q)
        q_high[slot] = high
        q_low[slot] = low

    def active(s):
        start = start_ref[s]
        span = span_ref[s]
        return ((row >= start) & (row < start + span)).astype(F32)

    def build_border(s, keep=None):
        build(4 + s, vec_border[s], fac_border[s], active(s), keep)

    def keep_lower(q):
        lower_send[...] = q[nb:]

    def keep_corner(q):
        corner_send[...] = q[nb:, nb:]

    load_border.wait()
    load_fac_border.wait()
    load_start.wait()
    load_span.wait()

    border_from_mate[0].wait_recv()
    build_border(0, keep_lower)
    lower_down.start()
    down_first[1].start()
    border_from_mate[1].wait_recv()
    build_border(2, keep_corner)
    corner_down.start()
    for copy in down_first[2:]:
        copy.start()
    load_inner.wait()
    load_fac_inner.wait()
    inner_from_mate.wait_recv()
    build(0, vec_inner[0], fac_inner[0], None)

    build_border(1)
    for slot in (1, 2, 3):
        build(slot, vec_inner[slot], fac_inner[slot], None)
    build_border(3)

    def q_of(slot, r=slice(None), c=slice(None)):
        return q_high[slot, r, c], q_low[slot, r, c]

    def apply(slot, band):
        return band - product(q_of(slot), halves(band))

    load_panel.wait()

    def span_of(k):
        return slice(k * chunk, (k + 1) * chunk)

    def lower_side(k):
        state[nb : 3 * nb, span_of(k)] = apply(0, state[nb : 3 * nb, span_of(k)])
        up_first[k].wait_recv()
        end = state[3 * nb :, span_of(k)]
        band = jnp.concatenate([end, below_first[k]], axis=0)
        end = end - product(q_of(4, slice(0, nb)), halves(band))
        band = jnp.concatenate([state[2 * nb : 3 * nb, span_of(k)], end], axis=0)
        band = apply(5, band)
        share[k] = product(q_of(6, slice(nb, None), slice(0, nb)), halves(band[nb:]))
        state[2 * nb :, span_of(k)] = band

    def upper_side(k):
        down_first[k].wait_recv()
        first = state[:nb, span_of(k)]
        band = jnp.concatenate([above_first[k], first], axis=0)
        first = first - product(halves(lower_all[...]), halves(band))
        band = jnp.concatenate([first, state[nb : 2 * nb, span_of(k)]], axis=0)
        band = apply(1, band)
        raise_buf[k] = band[:nb]
        state[: 2 * nb, span_of(k)] = band

    def middle(k):
        state[nb : 3 * nb, span_of(k)] = apply(2, state[nb : 3 * nb, span_of(k)])
        first = state[:nb, span_of(k)]
        state[:nb, span_of(k)] = first - product(halves(corner_all[...]), halves(first))

    def finish_upper(k):
        down_second[k].wait_recv()
        first = state[:nb, span_of(k)] - above_second[k]
        band = jnp.concatenate([first, state[nb : 2 * nb, span_of(k)]], axis=0)
        out[: 2 * nb, span_of(k)] = apply(3, band)

    def finish_lower(k):
        up_second[k].wait_recv()
        end = state[3 * nb :, span_of(k)]
        band = jnp.concatenate([end, below_second[k]], axis=0)
        end = end - product(q_of(6, slice(0, nb)), halves(band))
        band = jnp.concatenate([state[2 * nb : 3 * nb, span_of(k)], end], axis=0)
        out[2 * nb :, span_of(k)] = apply(7, band)

    def weights():
        lower_down.wait_recv()
        lower_pair.start()
        corner_down.wait_recv()
        corner_pair.start()
        lower_pair.wait_recv()
        corner_pair.wait_recv()

    def sent_down(k):
        down_second[k].start()

    def sent_up(k):
        up_second[k].start()

    def early():
        for k in range(CHUNKS):
            lower_side(k)
            sent_down(k)
        weights()
        for k in range(CHUNKS):
            upper_side(k)
            sent_up(k)

    def usual():
        for k in range(CHUNKS):
            lower_side(k)
            sent_down(k)
            if k == 0:
                weights()
            upper_side(k)
            sent_up(k)

    pl.when(top)(early)
    pl.when(jnp.logical_not(top))(usual)
    for k in range(CHUNKS):
        middle(k)
    finish_lower(0)
    for k in range(1, CHUNKS):
        finish_lower(k)
        finish_upper(k - 1)
    finish_upper(last)
    for copy in sends:
        copy.wait_send()


def local(panel, inner_vecs, inner_factor, border_vecs, border_factor, group_start, group_span, *, rows):
    height, width = panel.shape
    nb = height // 4
    chunk = width // CHUNKS
    steps = inner_factor.shape[1]
    vmem, dma = pltpu.VMEM, pltpu.SemaphoreType.DMA
    anywhere = pl.BlockSpec(memory_space=pl.ANY)
    copies = 4 * CHUNKS + 7
    operands = (
        panel,
        inner_vecs,
        inner_factor,
        border_vecs,
        border_factor,
        group_start,
        group_span,
    )
    result = pl.pallas_call(
        functools.partial(kernel, rows),
        out_shape=jax.ShapeDtypeStruct(panel.shape, F32),
        in_specs=[pl.BlockSpec(memory_space=pltpu.HBM)] * 7,
        out_specs=pl.BlockSpec(memory_space=pltpu.VMEM),
        scratch_shapes=[
            vmem((height, width), F32),
            vmem((steps, 2 * nb, nb), F32),
            vmem((steps, 2 * nb, nb), F32),
            vmem((steps, nb, nb), F32),
            vmem((steps, nb, nb), F32),
            vmem((2 * steps, 2 * nb, 2 * nb), BF16),
            vmem((2 * steps, 2 * nb, 2 * nb), BF16),
            vmem((nb, 2 * nb), F32),
            vmem((nb, 2 * nb), F32),
            vmem((nb, nb), F32),
            vmem((nb, nb), F32),
            vmem((CHUNKS, nb, chunk), F32),
            vmem((CHUNKS, nb, chunk), F32),
            vmem((CHUNKS, nb, chunk), F32),
            vmem((CHUNKS, nb, chunk), F32),
            vmem((CHUNKS, nb, chunk), F32),
            vmem((CHUNKS, nb, chunk), F32),
            pltpu.SMEM((steps,), jnp.int32),
            pltpu.SMEM((steps,), jnp.int32),
            dma((7,)),
            dma((copies,)),
            dma((copies,)),
        ],
        compiler_params=pltpu.CompilerParams(
            collective_id=0, has_side_effects=True, vmem_limit_bytes=48 * 2**20
        ),
        name="diamonds",
    )(*(pltpu.with_memory_space_constraint(a, pltpu.HBM) for a in operands))
    return result


def solution(mesh):
    placed = (
        P("row", "col"),
        P("row", None, "col", None),
        P("row", None, None, None),
        P("row", None, "col", None),
        P("row", None, None, None),
        P(),
        P(),
    )
    return jax.shard_map(
        functools.partial(local, rows=mesh.shape["row"]),
        mesh=mesh,
        in_specs=placed,
        out_specs=P("row", "col"),
        check_vma=False,
    )
```
